512 devices in a mesh: pair: 32 (over x, z), aux: 16 (over y, core).
Axes of the slice: x: 4, y: 8, z: 8, core: 2. Of those that a mesh axis runs over, the one named last changes fastest.
Arguments:
- amps: bfloat16 [4096, 128, 128], P(('pair', 'aux')), may hold values from -6 to 6
- rotation: bfloat16 [4096, 128, 128], P(('pair', 'aux')), may hold values from -0.5 to 0.5
- intersections: bfloat16 [4096, 4, 128, 128], P(('pair', 'aux')), may hold values from -0.5 to 0.5
- energies: float32 [4096, 128], P(('pair', 'aux')), may hold values from 0.25 to 2
- domains: int32 [4096, 2], P(('pair', 'aux')), may hold values from 0 to 31
- owners: int32 [4096, 4], P(('pair', 'aux')), may hold values from 0 to 31, all different within a row; in each aligned block of 8 rows (0 to 7, 8 to 15, ...) at most 2 rows name the same one
- slots: int32 [4096, 4], P(('pair', 'aux')), may hold values from 0 to 7
- tiles: int32 [4096], P(('pair', 'aux')), may hold values from 0 to 31
- blocks: bfloat16 [32, 512, 128], P('aux'), may hold values from -3 to 3
- coeffs: bfloat16 [32, 128, 4096], P('pair', None, 'aux'), may hold values from -0.5 to 0.5
Outputs:
- new_amps: bfloat16 [4096, 128, 128], P(('pair', 'aux'))
- density: float32 [32, 128, 4096], P('pair', None, 'aux')
The draws below stay inside these ranges and needn't reach their ends.
Inputs may be any that keep to these rules, and one draw needn't show every extreme that they name: Each row names distinct owners; among the rows of one device no owner is named by more than 2 entries, a bound that some block reaches.
All inputs are finite; a program needn't handle non-finite values.
Results may differ from the reference program's by a relative error of at most 0.014.
Values may be sent and summed in bfloat16 or wider, within the bound.
No kernel may reach another device: no remote copies, remote signals or barrier semaphores. Data moves between devices by JAX's collectives and lax.ppermute only.
A program may use at most 64 MiB of HBM per device.

```python
import math
import jax
import jax.numpy as jnp
import numpy as np
from jax import lax

VIRTUALS = 128
AUX_FUNCS = 512
AO_WIDTH = 4096
NEIGHBOURS = 4
PAIR_DEV = 8
PAIRS = 4096
CAPACITY = 2
BLOCKS = 32
TILES = 32
N_PAIR = 32
N_AUX = 16


def with_ends(values, rng, smallest, top_value):
    longest = values.shape.index(max(values.shape))
    spots = []
    for shift in (0, 1):
        where = [jax.random.randint(jax.random.fold_in(rng, axis), (), 0, length) for axis, length in enumerate(values.shape)]
        where[longest] = (where[longest] + shift) % values.shape[longest]
        spots.append(tuple(where))
    return values.at[spots[0]].set(smallest).at[spots[1]].set(top_value)


def block_levels(rng, dims, pieces, smallest, largest):
    def one(dim, shards_of):
        heights = jax.random.uniform(jax.random.fold_in(jax.random.fold_in(rng, 6), dim), (shards_of,), jnp.float32, smallest / len(pieces), largest / len(pieces))
        return jnp.repeat(jnp.exp(heights), dims[dim] // shards_of).reshape((-1,) + (1,) * (len(dims) - dim - 1))

    factor_of = one(*pieces[0])
    for cut in pieces[1:]:
        factor_of = factor_of * one(*cut)
    return factor_of


def assign_block(rng, own, number, rows, number_of, top, limit, slope):
    sequence = jax.random.permutation(rng, number_of)
    packed, common = shares(number_of, rows * top, limit, slope, True), shares(number_of, rows * top, limit, slope, False)
    places = jnp.arange(number_of)

    def named(lengths, offset_by):
        used = int((lengths > 0).sum())
        fixed = max(1, used // 4)
        shifted = fixed + (places - fixed + offset_by * (used - fixed)) % max(1, number_of - fixed)
        return jnp.zeros((number_of,), jnp.int32).at[sequence[jnp.where(places < fixed, places, shifted)]].set(jnp.asarray(lengths, jnp.int32))

    lengths = jnp.where(number % 4 == 0, named(packed, number // 4), named(common, number - number // 4 - 1))
    mixed = jax.random.permutation(jax.random.fold_in(own, 3), number_of)
    giver, receiver = mixed[0:number_of // 2 * 2:2], mixed[1:number_of // 2 * 2:2]
    room = jnp.minimum(lengths[giver] - 1, limit - lengths[receiver]) // 2
    room = jnp.where((giver == sequence[0]) | (receiver == sequence[0]) | (lengths[receiver] == 0), 0, jnp.maximum(room, 0))
    shifted = jax.random.randint(jax.random.fold_in(own, 4), (number_of // 2,), 0, 1 << 20) % (room + 1)
    lengths = lengths.at[giver].add(-shifted).at[receiver].add(shifted)
    members = jnp.searchsorted(jnp.cumsum(lengths), jnp.arange(rows * top), side="right").astype(jnp.int32)
    listing = members.reshape(top, rows).T
    listing = listing[jax.random.permutation(jax.random.fold_in(own, 1), rows)]
    offset_by = jax.random.randint(jax.random.fold_in(own, 2), (rows, 1), 0, top)
    return jnp.take_along_axis(listing, (jnp.arange(top)[None, :] + offset_by) % top, axis=1)


def shares(number_of, total, most, skew, full):
    loads = [(1 << 20) // math.isqrt(rank ** skew) + 1 for rank in range(1, number_of + 1)]
    largest = most if full else min(most, max(-(-total // number_of), total * loads[0] // sum(loads)))
    least = 1 if total - largest >= number_of - 1 else 0
    counts, rest = [largest] + [least] * (number_of - 1), total - largest - least * (number_of - 1)
    while rest > 0:
        free = [i for i in range(1, number_of) if counts[i] < largest] or [i for i in range(1, number_of) if counts[i] < most]
        pool, remaining = sum([loads[i] for i in free]), rest
        for i in free:
            addition = min(most - counts[i], max(1, remaining * loads[i] // pool), rest)
            counts[i] = counts[i] + addition
            rest = rest - addition
    return np.array(counts)


def scatter_about(key, dims, spread, limit, shards=(), kind=jnp.bfloat16):
    level = block_levels(key, dims, shards, -0.22, 0.18) if shards else 1.0
    drawn = jax.random.normal(key, dims, jnp.float32) * spread * level
    return jnp.minimum(jnp.maximum(drawn, -limit), limit).astype(kind)


def setup_inputs(seed: int = 0) -> dict:
    key_list = jax.random.split(jax.random.key(seed), 11)
    amps = scatter_about(key_list[0], (PAIRS, VIRTUALS, VIRTUALS), 1.0, 6.0, ((0, 512),))
    rotation = scatter_about(key_list[1], (PAIRS, VIRTUALS, VIRTUALS), VIRTUALS ** -0.5, 0.5, ((0, 512),))
    intersections = scatter_about(key_list[2], (PAIRS, NEIGHBOURS, VIRTUALS, VIRTUALS), VIRTUALS ** -0.5, 0.5, ((0, 512),))
    energies = jnp.clip(jnp.exp(math.log(2.0) - 2.0794415 * jax.random.uniform(key_list[3], (PAIRS, VIRTUALS), jnp.float32) ** block_levels(key_list[3], (PAIRS, VIRTUALS), ((0, 512),), -0.2, 0.2)), 0.25, 2.0)
    domains = with_ends(jax.random.randint(key_list[4], (PAIRS, 2), 0, BLOCKS), jax.random.fold_in(key_list[4], 1), 0, BLOCKS - 1).astype(jnp.int32)
    owners_keys = jax.random.split(jax.random.fold_in(key_list[5], 1), PAIRS // PAIR_DEV)
    owners_turns = jax.random.permutation(jax.random.fold_in(key_list[5], 3), PAIRS // PAIR_DEV)
    owners = jax.vmap(lambda own, number: assign_block(jax.random.fold_in(key_list[5], 2), own, number, PAIR_DEV, N_PAIR, NEIGHBOURS, CAPACITY, 2))(owners_keys, owners_turns).reshape((PAIRS, NEIGHBOURS))
    slots = with_ends(jax.random.randint(key_list[6], (PAIRS, NEIGHBOURS), 0, PAIR_DEV), jax.random.fold_in(key_list[6], 1), 0, PAIR_DEV - 1).astype(jnp.int32)
    tiles = with_ends(jax.random.randint(key_list[7], (PAIRS,), 0, TILES), jax.random.fold_in(key_list[7], 1), 0, TILES - 1).astype(jnp.int32)
    blocks = scatter_about(key_list[8], (BLOCKS, AUX_FUNCS, VIRTUALS), 0.21, 3.0, ((0, 16),))
    coeffs = scatter_about(key_list[9], (TILES, VIRTUALS, AO_WIDTH), VIRTUALS ** -0.5, 0.5, ((0, 32), (2, 16)))
    return dict(amps=amps, rotation=rotation, intersections=intersections, energies=energies, domains=domains, owners=owners, slots=slots, tiles=tiles, blocks=blocks, coeffs=coeffs)


def reference(amps, rotation, intersections, energies, domains, owners, slots, tiles, blocks, coeffs):
    pairs = PAIR_DEV * N_PAIR * N_AUX
    groups = N_PAIR * N_AUX
    column = ((jnp.arange(pairs, dtype=jnp.int32) // PAIR_DEV) % N_AUX).astype(jnp.int32)
    target = ((owners * N_AUX + column[:, None]) * PAIR_DEV + slots).astype(jnp.int32)

    def grouped(value):
        return value.reshape((groups, PAIR_DEV) + value.shape[1:])

    def push_step(carry, inputs):
        amp_b, over_b, target_b = inputs
        half_push = jnp.einsum("pnba,pbc->pnac", over_b.astype(jnp.float32), amp_b.astype(jnp.float32)).astype(jnp.bfloat16)
        sent_blocks = jnp.einsum("pnac,pncd->pnad", half_push.astype(jnp.float32), over_b.astype(jnp.float32)).astype(jnp.bfloat16)
        carry = carry.at[target_b.reshape(-1)].add(sent_blocks.reshape(-1, VIRTUALS, VIRTUALS).astype(jnp.float32))
        return carry, None

    incoming_all, _ = lax.scan(push_step, jnp.zeros((pairs, VIRTUALS, VIRTUALS), jnp.float32),
                               (grouped(amps), grouped(intersections), grouped(target)))

    def update_step(carry, inputs):
        amp_b, rot_b, over_b, pair_energy_backward, domain_b, target_b, tile_b, incoming_b = inputs
        left_block = jnp.take(blocks, domain_b[:, 0], axis=0).astype(jnp.float32)
        right_density_block = jnp.take(blocks, domain_b[:, 1], axis=0).astype(jnp.float32)
        rot_f = rot_b.astype(jnp.float32)
        left_fit = jnp.einsum("pqa,pab->pqb", left_block, rot_f).astype(jnp.bfloat16)
        right_fit = jnp.einsum("pqa,pab->pqb", right_density_block, rot_f).astype(jnp.bfloat16)
        integrals = jnp.einsum("pqa,pqb->pab", left_fit.astype(jnp.float32), right_fit.astype(jnp.float32))
        partner = jnp.take(amps, target_b.reshape(-1), axis=0).reshape(PAIR_DEV, NEIGHBOURS, VIRTUALS, VIRTUALS)
        over_f = over_b.astype(jnp.float32)
        half_gathered = jnp.einsum("pnab,pnbc->pnac", over_f, partner.astype(jnp.float32)).astype(jnp.bfloat16)
        pulled = jnp.einsum("pnac,pndc->pad", half_gathered.astype(jnp.float32), over_f)
        denom = pair_energy_backward[:, :, None] + pair_energy_backward[:, None, :]
        amp_f = amp_b.astype(jnp.float32)
        residual = integrals + denom * amp_f - pulled - incoming_b
        new_b = (amp_f - residual / (denom + 1.0)).astype(jnp.bfloat16)
        new_f = new_b.astype(jnp.float32)
        pair_density = (jnp.einsum("pab,pcb->pac", new_f, new_f) * (1.0 / VIRTUALS)).astype(jnp.bfloat16)
        rotated = jnp.einsum("pab,pbc->pac", rot_f, pair_density.astype(jnp.float32)).astype(jnp.bfloat16)
        tile_density = jnp.einsum("pac,pdc->pad", rotated.astype(jnp.float32), rot_f)
        carry = carry.at[tile_b].add(tile_density)
        return carry, new_b

    tile_accumulated, new_blocks = lax.scan(update_step, jnp.zeros((TILES, VIRTUALS, VIRTUALS), jnp.float32),
                                    (grouped(amps), grouped(rotation), grouped(intersections), grouped(energies),
                                     grouped(domains), grouped(target), grouped(tiles), grouped(incoming_all)))
    new_amps = new_blocks.reshape(pairs, VIRTUALS, VIRTUALS)
    density = jnp.einsum("vsi,vik->vsk", tile_accumulated, coeffs.astype(jnp.float32),
                         precision=lax.Precision.HIGHEST) * (1.0 / (PAIR_DEV * N_AUX))
    return new_amps, density
```

```python
import jax
import jax.numpy as jnp
from jax import lax
from jax.experimental import pallas as pl
from jax.experimental.pallas import tpu as pltpu
from jax.sharding import PartitionSpec as P


F32 = jnp.float32
BF16 = jnp.bfloat16
CAP = 2
SUB = 8
CORES = 2
VMEM = pl.BlockSpec(memory_space=pltpu.VMEM)
SMEM = pl.BlockSpec(memory_space=pltpu.SMEM)
HBM = pl.BlockSpec(memory_space=pltpu.HBM)
PLACE = (0, 4, 2, 7, 1, 5, 3, 6)


def mm(a, b, ca=1, cb=0):
    return lax.dot_general(a, b, (((ca,), (cb,)), ((), ())), preferred_element_type=F32)


def call(kernel, out_shape, in_specs, out_specs, args, flops, bytes_accessed, scratch=(), mib=12):
    return pl.pallas_call(
        kernel,
        out_shape=out_shape,
        in_specs=in_specs,
        out_specs=out_specs,
        scratch_shapes=list(scratch),
        compiler_params=pltpu.CompilerParams(vmem_limit_bytes=mib << 20),
        cost_estimate=pl.CostEstimate(
            flops=flops, bytes_accessed=bytes_accessed, transcendentals=0
        ),
    )(*args)


def push_kernel(owner_ref, slot_ref, amps_ref, inter_ref, send_ref, pos_ref, *scratch):
    block_buf, note_buf, count, first, sems, note_sem = scratch
    pairs, neighbours, v, _ = inter_ref.shape
    group = send_ref.shape[0]
    step = 2
    row = lax.broadcasted_iota(jnp.int32, (SUB, v), 0)
    note_buf[...] = jnp.zeros(note_buf.shape, BF16)

    @pl.loop(0, group)
    def _(o):
        count[o] = 0
        first[o] = 0

    @pl.loop(0, pairs)
    def _(p):
        for n in range(neighbours):
            o = owner_ref[n, p]
            s = slot_ref[n, p] + 1
            r = count[o]
            count[o] = r + 1
            f = jnp.where(r == 0, s, first[o])
            first[o] = f
            pos_ref[p * neighbours + n] = o * CAP + r
            second = jnp.where(r == 0, 0, s)
            note = jnp.where(row == 0, f, jnp.where(row == 1, second, 0))
            note_buf[o] = note.astype(F32).astype(BF16)

    def put(e):
        at = pos_ref[e]
        rows = pl.ds(pl.multiple_of(lax.rem(at, CAP) * v, v), v)
        return pltpu.make_async_copy(
            block_buf.at[e], send_ref.at[at // CAP, rows, :], sems.at[e]
        )

    def put_notes():
        return pltpu.make_async_copy(note_buf, send_ref.at[:, pl.ds(CAP * v, SUB), :], note_sem)

    def put_all(g):
        for i in range(step * neighbours):
            put(g * step * neighbours + i).start()

    @pl.loop(0, pairs // step)
    def _(g):
        overs = [[inter_ref[g * step + i, n] for n in range(neighbours)] for i in range(step)]
        halves = [
            mm(jnp.concatenate(overs[i], axis=1), amps_ref[g * step + i], 0, 0).astype(BF16)
            for i in range(step)
        ]
        for i in range(step):
            for n in range(neighbours):
                block = mm(halves[i][n * v : (n + 1) * v, :], overs[i][n]).astype(BF16)
                block_buf[(g * step + i) * neighbours + n] = block

        @pl.when(g > 0)
        def _():
            put_all(g - 1)

    put_notes().start()
    put_all(pairs // step - 1)
    put_notes().wait()

    @pl.loop(0, pairs * neighbours)
    def _(e):
        put(e).wait()


def reply_kernel(info_ref, amps_ref, out_ref, sems):
    group = out_ref.shape[0]

    def put(d, r):
        s = jnp.maximum(info_ref[d, r] - 1, 0)
        return pltpu.make_async_copy(amps_ref.at[s], out_ref.at[d, r], sems.at[d, r])

    @pl.loop(0, group)
    def _(d):
        for r in range(CAP):
            put(d, r).start()

    @pl.loop(0, group)
    def _(d):
        for r in range(CAP):
            put(d, r).wait()


def incoming_kernel(info_ref, recv_ref, out_ref):
    group = recv_ref.shape[0]
    v = out_ref.shape[1]
    out_ref[...] = jnp.zeros(out_ref.shape, F32)

    @pl.loop(0, group)
    def _(d):
        for r in range(CAP):
            s = info_ref[d, r]

            @pl.when(s > 0)
            def _():
                out_ref[s - 1] += recv_ref[d, r * v : (r + 1) * v, :].astype(F32)


def denominator(energy_ref, p):
    v = energy_ref.shape[1]
    across = jnp.broadcast_to(energy_ref[pl.ds(p, 1), :], (v, v))
    return across.T + across


def integral_kernel(
    domain_ref, me_ref, own_ref, other_ref, rot_ref, amps_ref, energy_ref, incoming_ref, out_ref
):
    pairs = rot_ref.shape[0]
    per = own_ref.shape[0] // len(PLACE)
    chip = me_ref[0] // CORES
    core = lax.rem(me_ref[0], CORES)

    @pl.loop(0, pairs)
    def _(p):
        rot = rot_ref[p]

        def block(side):
            d = domain_ref[side, p]
            device = d // per
            back = lax.rem(chip - device // CORES + len(PLACE), len(PLACE))
            place = jnp.int32(PLACE[0])
            for k in range(1, len(PLACE)):
                place = jnp.where(back == k, PLACE[k], place)
            at = place * per + lax.rem(d, per)
            same = (lax.rem(device, CORES) == core).astype(jnp.int32)
            pick = jnp.full((1, 1), same) > 0
            return jnp.where(pick, own_ref[at], other_ref[at])

        left = mm(rot, block(0), 0, 1).astype(BF16)
        right = mm(block(1), rot).astype(BF16)
        amp = amps_ref[p].astype(F32)
        out_ref[p] = mm(left, right) + denominator(energy_ref, p) * amp - incoming_ref[p]


def update_kernel(
    pos_ref, arrived_ref, inter_ref, amps_ref, rot_ref, energy_ref, base_ref, note_ref,
    new_ref, out_ref, part, sems,
):
    pairs, neighbours, v, _ = inter_ref.shape
    slabs = out_ref.shape[0]
    step = 4

    def get(e):
        return pltpu.make_async_copy(arrived_ref.at[pos_ref[e]], part.at[e], sems.at[e])

    @pl.loop(0, pairs * neighbours)
    def _(e):
        get(e).start()

    for r in range(slabs):
        out_ref[r, pairs] = note_ref[...]

    @pl.loop(0, pairs // step)
    def _(g):
        at = [g * step + i for i in range(step)]
        for p in at:
            for n in range(neighbours):
                get(p * neighbours + n).wait()
        halves = [
            [
                mm(inter_ref[p, n], part[p * neighbours + n]).astype(BF16)
                for n in range(neighbours)
            ]
            for p in at
        ]
        pulled = [
            mm(
                jnp.concatenate(half, axis=1),
                jnp.concatenate([inter_ref[p, n] for n in range(neighbours)], axis=1),
                1,
                1,
            )
            for p, half in zip(at, halves)
        ]
        news = []
        for p, pull in zip(at, pulled):
            residual = base_ref[p] - pull
            amp = amps_ref[p].astype(F32)
            news.append((amp - residual / (denominator(energy_ref, p) + 1.0)).astype(BF16))
        densities = [(mm(new, new, 1, 1) * (1.0 / v)).astype(BF16) for new in news]
        rots = [mm(rot_ref[p], d).astype(BF16) for p, d in zip(at, densities)]
        for p, new, rotated in zip(at, news, rots):
            new_ref[p] = new
            tile = mm(rotated, rot_ref[p], 1, 1).astype(BF16)
            for r in range(slabs):
                out_ref[r, p] = tile[r * SUB : (r + 1) * SUB, :]


def slab_kernel(recv_ref, out_ref, wide, total):
    sources, blocks, _, v = recv_ref.shape
    pairs = blocks - 1
    count = out_ref.shape[0]
    wide[...] = recv_ref[:, :pairs].astype(F32).reshape(wide.shape)
    ids = jnp.sum(recv_ref[:, pairs].astype(F32), axis=0)[0:1, :]
    which = lax.broadcasted_iota(jnp.int32, (count, sources * pairs), 0).astype(F32)
    hot = (which == ids).astype(F32).astype(BF16)
    for s in range(SUB):
        rows = wide[pl.ds(s, sources * pairs, stride=SUB), :].astype(BF16)
        total[:, s, :] = mm(hot, rows)
    out_ref[...] = total[...].astype(BF16)


def local(amps, rotation, intersections, energies, domains, owners, slots, tiles, blocks, coeffs):
    pairs, v, _ = amps.shape
    neighbours = owners.shape[1]
    group = lax.axis_size("pair")
    ring = lax.axis_size("aux")
    chips = ring // CORES
    entries = pairs * neighbours
    cube = v * v
    me = lax.axis_index("aux").astype(jnp.int32)

    assert chips == len(PLACE)

    def shift(value, k):
        return lax.ppermute(
            value, "aux", [(j, (j + CORES * k) % ring) for j in range(ring)]
        )

    far = [blocks, shift(blocks, 4), shift(blocks, 2), shift(blocks, -2)]

    send, position = call(
        push_kernel,
        (
            jax.ShapeDtypeStruct((group, CAP * v + SUB, v), BF16),
            jax.ShapeDtypeStruct((entries,), jnp.int32),
        ),
        [SMEM, SMEM, VMEM, VMEM],
        (HBM, SMEM),
        (owners.T, slots.T, amps, intersections),
        4 * entries * cube * v,
        2 * cube * (pairs + entries + group * CAP),
        [
            pltpu.VMEM((entries, v, v), BF16),
            pltpu.VMEM((group, SUB, v), BF16),
            pltpu.SMEM((group,), jnp.int32),
            pltpu.SMEM((group,), jnp.int32),
            pltpu.SemaphoreType.DMA((entries,)),
            pltpu.SemaphoreType.DMA,
        ],
    )
    recv = lax.all_to_all(send, "pair", 0, 0, tiled=True)
    info = recv[:, CAP * v : CAP * v + CAP, 0].astype(jnp.int32)
    info, *far = lax.optimization_barrier((info, *far))
    two = jnp.concatenate(far[:2], axis=0)
    reply = call(
        reply_kernel,
        jax.ShapeDtypeStruct((group, CAP, v, v), BF16),
        [SMEM, VMEM],
        HBM,
        (info, amps),
        0,
        2 * cube * (pairs + group * CAP),
        [pltpu.SemaphoreType.DMA((group, CAP))],
    )
    arrived = lax.all_to_all(reply, "pair", 0, 0, tiled=True)
    incoming = call(
        incoming_kernel,
        jax.ShapeDtypeStruct((pairs, v, v), F32),
        [SMEM, VMEM],
        VMEM,
        (info, recv),
        group * CAP * cube,
        2 * cube * group * CAP,
    )
    own = jnp.concatenate([*far, shift(two, 1), shift(two, -1)], axis=0)
    other = lax.ppermute(own, "aux", [(j, j ^ 1) for j in range(ring)])
    base = call(
        integral_kernel,
        jax.ShapeDtypeStruct((pairs, v, v), F32),
        [SMEM, SMEM] + [VMEM] * 6,
        VMEM,
        (domains.T, me.reshape(1), own, other, rotation, amps, energies, incoming),
        6 * pairs * blocks.shape[1] * cube,
        4 * own.size,
    )
    lane = jnp.arange(ring * pairs, dtype=jnp.int32)
    spread = jnp.where(lane // pairs == me, jnp.tile(tiles, ring), 0).astype(BF16)
    note = jnp.broadcast_to(spread[None, :], (SUB, ring * pairs))
    new_amps, slabs = call(
        update_kernel,
        (
            jax.ShapeDtypeStruct((pairs, v, v), BF16),
            jax.ShapeDtypeStruct((ring, pairs + 1, SUB, v), BF16),
        ),
        [SMEM, pl.BlockSpec(memory_space=pl.ANY)] + [VMEM] * 6,
        (VMEM, VMEM),
        (
            position, arrived.reshape(group * CAP, v, v), intersections, amps, rotation, energies,
            base, note,
        ),
        (4 * entries + 6 * pairs) * cube * v,
        2 * cube * (2 * entries + 8 * pairs),
        [pltpu.VMEM((entries, v, v), BF16), pltpu.SemaphoreType.DMA((entries,))],
    )
    gathered = lax.all_to_all(slabs, "aux", 0, 0, tiled=True)
    tile_count = coeffs.shape[0] * group
    partial_sum = call(
        slab_kernel,
        jax.ShapeDtypeStruct((tile_count, SUB, v), BF16),
        [VMEM],
        VMEM,
        (gathered,),
        2 * tile_count * ring * pairs * SUB * v,
        4 * gathered.size,
        [pltpu.VMEM((ring * pairs * SUB, v), F32), pltpu.VMEM((tile_count, SUB, v), F32)],
    )
    spread_sum = lax.all_to_all(partial_sum, "pair", 0, 0, tiled=True)
    slab = jnp.sum(spread_sum.astype(F32), axis=0).astype(BF16)
    whole = lax.all_to_all(
        jnp.broadcast_to(slab[None], (ring, SUB, v)), "aux", 0, 0, tiled=True
    ).reshape(v, v)
    factor = 1.0 / (pairs * ring)
    density = jnp.dot(whole, coeffs[0], preferred_element_type=F32) * factor
    return (new_amps, density[None])


def solution(mesh):
    return jax.shard_map(
        local,
        mesh=mesh,
        in_specs=(
            P(("pair", "aux"), None, None),
            P(("pair", "aux"), None, None),
            P(("pair", "aux"), None, None, None),
            P(("pair", "aux"), None),
            P(("pair", "aux"), None),
            P(("pair", "aux"), None),
            P(("pair", "aux"), None),
            P(("pair", "aux")),
            P("aux", None, None),
            P("pair", None, "aux"),
        ),
        out_specs=(P(("pair", "aux"), None, None), P("pair", None, "aux")),
        check_vma=False,
    )
```

```python
import jax
import jax.numpy as jnp
from jax import lax
from jax.experimental import pallas as pl
from jax.experimental.pallas import tpu as pltpu
from jax.sharding import Mesh
from jax.sharding import PartitionSpec as P


F32 = jnp.float32
BF16 = jnp.bfloat16
CAP = 2
PAIR = ("x", "z")
AUX = ("y", "core")
FINE = (4, 8, 8, 2)
SUB = 8
CORES = 2
VMEM = pl.BlockSpec(memory_space=pltpu.VMEM)
SMEM = pl.BlockSpec(memory_space=pltpu.SMEM)
HBM = pl.BlockSpec(memory_space=pltpu.HBM)
PLACE = (0, 4, 2, 7, 1, 5, 3, 6)


def mm(a, b, ca=1, cb=0):
    return lax.dot_general(a, b, (((ca,), (cb,)), ((), ())), preferred_element_type=F32)


def call(kernel, out_shape, in_specs, out_specs, args, flops, bytes_accessed, scratch=(), mib=12):
    return pl.pallas_call(
        kernel,
        out_shape=out_shape,
        in_specs=in_specs,
        out_specs=out_specs,
        scratch_shapes=list(scratch),
        compiler_params=pltpu.CompilerParams(vmem_limit_bytes=mib << 20),
        cost_estimate=pl.CostEstimate(
            flops=flops, bytes_accessed=bytes_accessed, transcendentals=0
        ),
    )(*args)


def plan_kernel(owner_ref, slot_ref, want_ref, pos_ref, count):
    neighbours, pairs = owner_ref.shape
    rows, width = want_ref.shape

    @pl.loop(0, rows)
    def _(o):
        for i in range(width):
            want_ref[o, i] = 0
        for i in range(width // CAP):
            count[o * (width // CAP) + i] = 0

    @pl.loop(0, pairs)
    def _(p):
        for n in range(neighbours):
            o = owner_ref[n, p]
            r = count[o]
            count[o] = r + 1
            at = o * CAP + r
            pos_ref[p * neighbours + n] = at
            want_ref[at // width, lax.rem(at, width)] = slot_ref[n, p] + 1


def push_kernel(pos_ref, amps_ref, inter_ref, send_ref, *scratch):
    amps_buf, inter_buf, block_buf, sems, amps_sems, inter_sems = scratch
    pairs, neighbours, v, _ = inter_ref.shape
    step = 2

    def get(p):
        return (
            pltpu.make_async_copy(amps_ref.at[p], amps_buf.at[p], amps_sems.at[p]),
            pltpu.make_async_copy(inter_ref.at[p], inter_buf.at[p], inter_sems.at[p]),
        )

    def put(e):
        return pltpu.make_async_copy(block_buf.at[e], send_ref.at[pos_ref[e]], sems.at[e])

    def put_all(g):
        for i in range(step * neighbours):
            put(g * step * neighbours + i).start()

    for p in range(pairs):
        for copy in get(p):
            copy.start()

    @pl.loop(0, pairs // step)
    def _(g):
        for i in range(step):
            for copy in get(g * step + i):
                copy.wait()
        overs = [[inter_buf[g * step + i, n] for n in range(neighbours)] for i in range(step)]
        halves = [
            mm(jnp.concatenate(overs[i], axis=1), amps_buf[g * step + i], 0, 0).astype(BF16)
            for i in range(step)
        ]
        for i in range(step):
            for n in range(neighbours):
                block = mm(halves[i][n * v : (n + 1) * v, :], overs[i][n]).astype(BF16)
                block_buf[(g * step + i) * neighbours + n] = block

        @pl.when(g > 0)
        def _():
            put_all(g - 1)

    put_all(pairs // step - 1)

    @pl.loop(0, pairs * neighbours)
    def _(e):
        put(e).wait()


def reply_kernel(want_ref, held_ref, out_ref):
    rows, width = want_ref.shape
    per = held_ref.shape[0] // (width // CAP)

    @pl.loop(0, rows)
    def _(d):
        for i in range(width):
            out_ref[d, i] = held_ref[i // CAP * per + jnp.maximum(want_ref[d, i] - 1, 0)]


def sum_kernel(want_ref, recv_ref, out_ref, total):
    rows, width = want_ref.shape
    per = total.shape[0]

    @pl.loop(0, width // CAP)
    def _(o):
        total[...] = jnp.zeros(total.shape, F32)
        for d in range(rows):
            for r in range(CAP):
                s = want_ref[d, o * CAP + r]

                @pl.when(s > 0)
                def _():
                    total[s - 1] += recv_ref[d, o * CAP + r].astype(F32)

        out_ref[pl.ds(o * per, per)] = total[...].astype(BF16)


def denominator(energy_ref, p):
    v = energy_ref.shape[1]
    across = jnp.broadcast_to(energy_ref[pl.ds(p, 1), :], (v, v))
    return across.T + across


def integral_kernel(
    domain_ref, me_ref, own_ref, other_ref, rot_ref, amps_ref, energy_ref, out_ref
):
    pairs = rot_ref.shape[0]
    per = own_ref.shape[0] // len(PLACE)
    chip = me_ref[0] // CORES
    core = lax.rem(me_ref[0], CORES)

    @pl.loop(0, pairs)
    def _(p):
        rot = rot_ref[p]

        def block(side):
            d = domain_ref[side, p]
            device = d // per
            back = lax.rem(chip - device // CORES + len(PLACE), len(PLACE))
            place = jnp.int32(PLACE[0])
            for k in range(1, len(PLACE)):
                place = jnp.where(back == k, PLACE[k], place)
            at = place * per + lax.rem(d, per)
            same = (lax.rem(device, CORES) == core).astype(jnp.int32)
            pick = jnp.full((1, 1), same) > 0
            return jnp.where(pick, own_ref[at], other_ref[at])

        left = mm(rot, block(0), 0, 1).astype(BF16)
        right = mm(block(1), rot).astype(BF16)
        amp = amps_ref[p].astype(F32)
        out_ref[p] = mm(left, right) + denominator(energy_ref, p) * amp


def pull_kernel(pos_ref, arrived_ref, inter_ref, out_ref, part, sems):
    pairs, neighbours, _, _ = inter_ref.shape
    step = 4

    def get(e):
        return pltpu.make_async_copy(arrived_ref.at[pos_ref[e]], part.at[e], sems.at[e])

    @pl.loop(0, pairs * neighbours)
    def _(e):
        get(e).start()

    @pl.loop(0, pairs // step)
    def _(g):
        at = [g * step + i for i in range(step)]
        for p in at:
            for n in range(neighbours):
                get(p * neighbours + n).wait()
        halves = [
            [
                mm(inter_ref[p, n], part[p * neighbours + n]).astype(BF16)
                for n in range(neighbours)
            ]
            for p in at
        ]
        for p, half in zip(at, halves):
            out_ref[p] = mm(
                jnp.concatenate(half, axis=1),
                jnp.concatenate([inter_ref[p, n] for n in range(neighbours)], axis=1),
                1,
                1,
            )


def update_kernel(
    incoming_ref, amps_ref, rot_ref, energy_ref, base_ref, pulled_ref, note_ref, new_ref, out_ref
):
    pairs, v, _ = amps_ref.shape
    slabs = out_ref.shape[0]
    step = 4

    for r in range(slabs):
        out_ref[r, pairs] = note_ref[...]

    @pl.loop(0, pairs // step)
    def _(g):
        at = [g * step + i for i in range(step)]
        news = []
        for p in at:
            residual = base_ref[p] - pulled_ref[p] - incoming_ref[p].astype(F32)
            amp = amps_ref[p].astype(F32)
            news.append((amp - residual / (denominator(energy_ref, p) + 1.0)).astype(BF16))
        densities = [(mm(new, new, 1, 1) * (1.0 / v)).astype(BF16) for new in news]
        rots = [mm(rot_ref[p], d).astype(BF16) for p, d in zip(at, densities)]
        for p, new, rotated in zip(at, news, rots):
            new_ref[p] = new
            tile = mm(rotated, rot_ref[p], 1, 1).astype(BF16)
            for r in range(slabs):
                out_ref[r, p] = tile[r * SUB : (r + 1) * SUB, :]


def slab_kernel(recv_ref, out_ref, wide, total):
    sources, blocks, _, _ = recv_ref.shape
    pairs = blocks - 1
    count = out_ref.shape[0]
    wide[...] = recv_ref[:, :pairs].astype(F32).reshape(wide.shape)
    ids = jnp.sum(recv_ref[:, pairs].astype(F32), axis=0)[0:1, :]
    which = lax.broadcasted_iota(jnp.int32, (count, sources * pairs), 0).astype(F32)
    hot = (which == ids).astype(F32).astype(BF16)
    for s in range(SUB):
        rows = wide[pl.ds(s, sources * pairs, stride=SUB), :].astype(BF16)
        total[:, s, :] = mm(hot, rows)
    out_ref[...] = total[...].astype(BF16)


def local(amps, rotation, intersections, energies, domains, owners, slots, tiles, blocks, coeffs):
    pairs, v, _ = amps.shape
    neighbours = owners.shape[1]
    group = lax.axis_size(PAIR)
    ring = lax.axis_size(AUX)
    chips = ring // CORES
    entries = pairs * neighbours
    cube = v * v
    me = lax.axis_index(AUX).astype(jnp.int32)

    assert chips == len(PLACE)

    def shift(value, k):
        return lax.ppermute(value, "y", [(j, (j + k) % chips) for j in range(chips)])

    opposite = shift(blocks, 4)
    above, below = shift(blocks, 2), shift(blocks, -2)
    column = lax.all_gather(amps, "z", axis=0, tiled=True)
    across = lax.axis_size("x")
    width = CAP * group // across
    want, position = call(
        plan_kernel,
        (
            jax.ShapeDtypeStruct((across, width), jnp.int32),
            jax.ShapeDtypeStruct((entries,), jnp.int32),
        ),
        [SMEM, SMEM],
        (SMEM, SMEM),
        (owners.T, slots.T),
        0,
        1024,
        [pltpu.SMEM((group,), jnp.int32)],
    )
    asked = lax.all_to_all(want, "x", 0, 0, tiled=True)
    send = call(
        push_kernel,
        jax.ShapeDtypeStruct((group * CAP, v, v), BF16),
        [SMEM, HBM, HBM],
        HBM,
        (position, amps, intersections),
        4 * entries * cube * v,
        2 * cube * (pairs + entries + group * CAP),
        [
            pltpu.VMEM((pairs, v, v), BF16),
            pltpu.VMEM((pairs, neighbours, v, v), BF16),
            pltpu.VMEM((entries, v, v), BF16),
            pltpu.SemaphoreType.DMA((entries,)),
            pltpu.SemaphoreType.DMA((pairs,)),
            pltpu.SemaphoreType.DMA((pairs,)),
        ],
        58,
    )
    send, asked = lax.optimization_barrier((send, asked))
    recv = lax.all_to_all(send.reshape(across, width, v, v), "x", 0, 0, tiled=True)
    recv, opposite = lax.optimization_barrier((recv, opposite))
    sums = call(
        sum_kernel,
        jax.ShapeDtypeStruct((group // across * pairs, v, v), BF16),
        [SMEM, VMEM],
        VMEM,
        (asked, recv),
        group * CAP * cube,
        2 * cube * group * CAP,
        [pltpu.VMEM((pairs, v, v), F32)],
    )
    incoming = lax.psum_scatter(sums, "z", scatter_dimension=0, tiled=True)
    column, sums = lax.optimization_barrier((column, sums))
    reply = call(
        reply_kernel,
        jax.ShapeDtypeStruct((across, width, v, v), BF16),
        [SMEM, VMEM],
        VMEM,
        (asked, column),
        0,
        2 * cube * (pairs + group * CAP),
    )
    reply, blocks, opposite = lax.optimization_barrier((reply, blocks, opposite))
    arrived = lax.all_to_all(reply, "x", 0, 0, tiled=True)
    two = jnp.concatenate([blocks, opposite], axis=0)
    own = jnp.concatenate(
        [two, above, below, shift(two, 1), shift(two, -1)],
        axis=0,
    )
    other = lax.ppermute(own, "core", [(0, 1), (1, 0)])
    base = call(
        integral_kernel,
        jax.ShapeDtypeStruct((pairs, v, v), F32),
        [SMEM, SMEM] + [VMEM] * 5,
        VMEM,
        (domains.T, me.reshape(1), own, other, rotation, amps, energies),
        6 * pairs * blocks.shape[1] * cube,
        4 * own.size,
    )
    pulled = call(
        pull_kernel,
        jax.ShapeDtypeStruct((pairs, v, v), F32),
        [SMEM, pl.BlockSpec(memory_space=pl.ANY), VMEM],
        VMEM,
        (position, arrived.reshape(group * CAP, v, v), intersections),
        4 * entries * cube * v,
        2 * cube * (2 * entries + 2 * pairs),
        [pltpu.VMEM((entries, v, v), BF16), pltpu.SemaphoreType.DMA((entries,))],
    )
    lane = jnp.arange(ring * pairs, dtype=jnp.int32)
    spread = jnp.where(lane // pairs == me, jnp.tile(tiles, ring), 0).astype(BF16)
    note = jnp.broadcast_to(spread[None, :], (SUB, ring * pairs))
    new_amps, slabs = call(
        update_kernel,
        (
            jax.ShapeDtypeStruct((pairs, v, v), BF16),
            jax.ShapeDtypeStruct((ring, pairs + 1, SUB, v), BF16),
        ),
        [VMEM] * 7,
        (VMEM, VMEM),
        (incoming, amps, rotation, energies, base, pulled, note),
        6 * pairs * cube * v,
        2 * cube * 10 * pairs,
    )
    gathered = lax.all_to_all(slabs, AUX, 0, 0, tiled=True)
    tile_count = coeffs.shape[0] * group
    partial_sum = call(
        slab_kernel,
        jax.ShapeDtypeStruct((tile_count, SUB, v), BF16),
        [VMEM],
        VMEM,
        (gathered,),
        2 * tile_count * ring * pairs * SUB * v,
        4 * gathered.size,
        [pltpu.VMEM((ring * pairs * SUB, v), F32), pltpu.VMEM((tile_count, SUB, v), F32)],
    )
    spread_sum = lax.all_to_all(partial_sum, PAIR, 0, 0, tiled=True)
    slab = jnp.sum(spread_sum.astype(F32), axis=0).astype(BF16)
    whole = lax.all_to_all(
        jnp.broadcast_to(slab[None], (ring, SUB, v)), AUX, 0, 0, tiled=True
    ).reshape(v, v)
    factor = 1.0 / (pairs * ring)
    density = jnp.dot(whole, coeffs[0], preferred_element_type=F32) * factor
    return (new_amps, density[None])


def solution(mesh):
    fine = Mesh(mesh.devices.reshape(FINE), PAIR + AUX)

    return jax.shard_map(
        local,
        mesh=fine,
        in_specs=(
            P(PAIR + AUX, None, None),
            P(PAIR + AUX, None, None),
            P(PAIR + AUX, None, None, None),
            P(PAIR + AUX, None),
            P(PAIR + AUX, None),
            P(PAIR + AUX, None),
            P(PAIR + AUX, None),
            P(PAIR + AUX),
            P(AUX, None, None),
            P(PAIR, None, AUX),
        ),
        out_specs=(P(PAIR + AUX, None, None), P(PAIR, None, AUX)),
        check_vma=False,
    )
```

```python
import jax
import jax.numpy as jnp
from jax import lax
from jax.experimental import pallas as pl
from jax.experimental.pallas import tpu as pltpu
from jax.sharding import Mesh
from jax.sharding import PartitionSpec as P


F32 = jnp.float32
BF16 = jnp.bfloat16
CAP = 2
PAIR = ("x", "z")
AUX = ("y", "core")
FINE = (4, 8, 8, 2)
SUB = 8
CORES = 2
VMEM = pl.BlockSpec(memory_space=pltpu.VMEM)
SMEM = pl.BlockSpec(memory_space=pltpu.SMEM)
HBM = pl.BlockSpec(memory_space=pltpu.HBM)
PLACE = (0, 4, 2, 7, 1, 5, 3, 6)


def mm(a, b, ca=1, cb=0):
    return lax.dot_general(a, b, (((ca,), (cb,)), ((), ())), preferred_element_type=F32)


def call(kernel, out_shape, in_specs, out_specs, args, flops, bytes_accessed, scratch=(), mib=12):
    return pl.pallas_call(
        kernel,
        out_shape=out_shape,
        in_specs=in_specs,
        out_specs=out_specs,
        scratch_shapes=list(scratch),
        compiler_params=pltpu.CompilerParams(vmem_limit_bytes=mib << 20),
        cost_estimate=pl.CostEstimate(
            flops=flops, bytes_accessed=bytes_accessed, transcendentals=0
        ),
    )(*args)


def push_kernel(owner_ref, slot_ref, amps_ref, inter_ref, send_ref, pos_ref, *scratch):
    amps_buf, inter_buf, block_buf, note_buf, count, sems, amps_sems, inter_sems, note_sem = scratch
    pairs, neighbours, v, _ = inter_ref.shape
    rows = send_ref.shape[0]
    width = send_ref.shape[1] // v
    step = 2

    def get(p):
        return (
            pltpu.make_async_copy(amps_ref.at[p], amps_buf.at[p], amps_sems.at[p]),
            pltpu.make_async_copy(inter_ref.at[p], inter_buf.at[p], inter_sems.at[p]),
        )

    for p in range(pairs):
        for copy in get(p):
            copy.start()

    def put(e):
        at = pos_ref[e]
        place = pl.ds(pl.multiple_of(lax.rem(at, width) * v, v), v)
        return pltpu.make_async_copy(
            block_buf.at[e], send_ref.at[at // width, place, :], sems.at[e]
        )

    def put_notes():
        return pltpu.make_async_copy(note_buf, send_ref.at[:, pl.ds(width * v, SUB), :], note_sem)

    def put_all(g):
        for i in range(step * neighbours):
            put(g * step * neighbours + i).start()

    note_buf[...] = jnp.zeros(note_buf.shape, BF16)
    lane = lax.broadcasted_iota(jnp.int32, (SUB, v), 1)

    @pl.loop(0, rows * width // CAP)
    def _(o):
        count[o] = 0

    @pl.loop(0, pairs)
    def _(p):
        for n in range(neighbours):
            o = owner_ref[n, p]
            r = count[o]
            count[o] = r + 1
            at = o * CAP + r
            pos_ref[p * neighbours + n] = at
            d = at // width
            mark = jnp.where(lane == lax.rem(at, width), slot_ref[n, p] + 1, 0)
            note_buf[d] = note_buf[d] + mark.astype(F32).astype(BF16)

    @pl.loop(0, pairs // step)
    def _(g):
        for i in range(step):
            for copy in get(g * step + i):
                copy.wait()
        overs = [[inter_buf[g * step + i, n] for n in range(neighbours)] for i in range(step)]
        halves = [
            mm(jnp.concatenate(overs[i], axis=1), amps_buf[g * step + i], 0, 0).astype(BF16)
            for i in range(step)
        ]
        for i in range(step):
            for n in range(neighbours):
                block = mm(halves[i][n * v : (n + 1) * v, :], overs[i][n]).astype(BF16)
                block_buf[(g * step + i) * neighbours + n] = block

        @pl.when(g > 0)
        def _():
            put_all(g - 1)

    put_notes().start()
    put_all(pairs // step - 1)
    put_notes().wait()

    @pl.loop(0, pairs * neighbours)
    def _(e):
        put(e).wait()


def reply_kernel(
    want_ref, me_ref, first_ref, own_ref, far_ref, up_ref, down_ref, up2_ref, down2_ref, out_ref, held
):
    rows, width = want_ref.shape
    depth = width // CAP
    low = first_ref.shape[0] // depth
    high = own_ref.shape[0]
    per = low + high
    pieces = [own_ref, far_ref, up_ref, down_ref, up2_ref, up2_ref, down2_ref, down2_ref]
    offsets = [0, 0, 0, 0, 0, high, 0, high]
    for z in range(depth):
        held[z * per : z * per + low] = first_ref[z * low : (z + 1) * low]
    for k in range(depth):
        z = lax.rem(me_ref[0] - k + depth, depth)
        p = PLACE[k]
        held[pl.ds(z * per + low, high)] = pieces[p][offsets[p] : offsets[p] + high]

    @pl.loop(0, rows)
    def _(d):
        for i in range(width):
            out_ref[d, i] = held[i // CAP * per + jnp.maximum(want_ref[d, i] - 1, 0)]


def sum_kernel(want_ref, recv_ref, out_ref, total):
    rows, width = want_ref.shape
    per, v, _ = total.shape

    @pl.loop(0, width // CAP)
    def _(o):
        total[...] = jnp.zeros(total.shape, F32)
        for d in range(rows):
            for r in range(CAP):
                s = want_ref[d, o * CAP + r]
                place = pl.ds(pl.multiple_of((o * CAP + r) * v, v), v)

                @pl.when(s > 0)
                def _():
                    total[s - 1] += recv_ref[d, place, :].astype(F32)

        out_ref[pl.ds(o * per, per)] = total[...].astype(BF16)


def denominator(energy_ref, p):
    v = energy_ref.shape[1]
    across = jnp.broadcast_to(energy_ref[pl.ds(p, 1), :], (v, v))
    return across.T + across


def integral_kernel(
    domain_ref, me_ref, own_ref, other_ref, rot_ref, amps_ref, energy_ref, out_ref
):
    pairs = rot_ref.shape[0]
    per = own_ref.shape[0] // len(PLACE)
    chip = me_ref[0] // CORES
    core = lax.rem(me_ref[0], CORES)

    @pl.loop(0, pairs)
    def _(p):
        rot = rot_ref[p]

        def block(side):
            d = domain_ref[side, p]
            device = d // per
            back = lax.rem(chip - device // CORES + len(PLACE), len(PLACE))
            place = jnp.int32(PLACE[0])
            for k in range(1, len(PLACE)):
                place = jnp.where(back == k, PLACE[k], place)
            at = place * per + lax.rem(d, per)
            same = (lax.rem(device, CORES) == core).astype(jnp.int32)
            pick = jnp.full((1, 1), same) > 0
            return jnp.where(pick, own_ref[at], other_ref[at])

        left = mm(rot, block(0), 0, 1).astype(BF16)
        right = mm(block(1), rot).astype(BF16)
        amp = amps_ref[p].astype(F32)
        out_ref[p] = mm(left, right) + denominator(energy_ref, p) * amp


def pull_kernel(pos_ref, arrived_ref, inter_ref, out_ref, part, sems):
    pairs, neighbours, _, _ = inter_ref.shape
    step = 4

    def get(e):
        return pltpu.make_async_copy(arrived_ref.at[pos_ref[e]], part.at[e], sems.at[e])

    @pl.loop(0, pairs * neighbours)
    def _(e):
        get(e).start()

    @pl.loop(0, pairs // step)
    def _(g):
        at = [g * step + i for i in range(step)]
        for p in at:
            for n in range(neighbours):
                get(p * neighbours + n).wait()
        halves = [
            [
                mm(inter_ref[p, n], part[p * neighbours + n]).astype(BF16)
                for n in range(neighbours)
            ]
            for p in at
        ]
        for p, half in zip(at, halves):
            out_ref[p] = mm(
                jnp.concatenate(half, axis=1),
                jnp.concatenate([inter_ref[p, n] for n in range(neighbours)], axis=1),
                1,
                1,
            )


def update_kernel(
    incoming_ref, amps_ref, rot_ref, energy_ref, base_ref, pulled_ref, note_ref, new_ref, out_ref
):
    pairs, v, _ = amps_ref.shape
    slabs = out_ref.shape[0]
    step = 4

    for r in range(slabs):
        out_ref[r, pairs] = note_ref[...]

    @pl.loop(0, pairs // step)
    def _(g):
        at = [g * step + i for i in range(step)]
        news = []
        for p in at:
            residual = base_ref[p] - pulled_ref[p] - incoming_ref[p].astype(F32)
            amp = amps_ref[p].astype(F32)
            news.append((amp - residual / (denominator(energy_ref, p) + 1.0)).astype(BF16))
        densities = [(mm(new, new, 1, 1) * (1.0 / v)).astype(BF16) for new in news]
        rots = [mm(rot_ref[p], d).astype(BF16) for p, d in zip(at, densities)]
        for p, new, rotated in zip(at, news, rots):
            new_ref[p] = new
            tile = mm(rotated, rot_ref[p], 1, 1).astype(BF16)
            for r in range(slabs):
                out_ref[r, p] = tile[r * SUB : (r + 1) * SUB, :]


def slab_kernel(recv_ref, out_ref, wide, total):
    sources, blocks, _, _ = recv_ref.shape
    pairs = blocks - 1
    count = out_ref.shape[0]
    wide[...] = recv_ref[:, :pairs].astype(F32).reshape(wide.shape)
    ids = jnp.sum(recv_ref[:, pairs].astype(F32), axis=0)[0:1, :]
    which = lax.broadcasted_iota(jnp.int32, (count, sources * pairs), 0).astype(F32)
    hot = (which == ids).astype(F32).astype(BF16)
    for s in range(SUB):
        rows = wide[pl.ds(s, sources * pairs, stride=SUB), :].astype(BF16)
        total[:, s, :] = mm(hot, rows)
    out_ref[...] = total[...].astype(BF16)


def local(amps, rotation, intersections, energies, domains, owners, slots, tiles, blocks, coeffs):
    pairs, v, _ = amps.shape
    neighbours = owners.shape[1]
    group = lax.axis_size(PAIR)
    ring = lax.axis_size(AUX)
    chips = ring // CORES
    entries = pairs * neighbours
    cube = v * v
    me = lax.axis_index(AUX).astype(jnp.int32)

    assert chips == len(PLACE)

    depth = lax.axis_size("z")
    assert depth == len(PLACE)

    def shift(value, axis, k):
        size = lax.axis_size(axis)
        return lax.ppermute(value, axis, [(j, (j + k) % size) for j in range(size)])

    opposite = shift(blocks, "y", 4)
    above, below = shift(blocks, "y", 2), shift(blocks, "y", -2)
    low = pairs // 2
    column = lax.all_gather(amps[:low], "z", axis=0, tiled=True)
    high = amps[low:]
    zfar = shift(high, "z", 4)
    zup2, zdown2 = shift(high, "z", 2), shift(high, "z", -2)
    both = jnp.concatenate([high, zfar], axis=0)
    zup1, zdown1 = shift(both, "z", 1), shift(both, "z", -1)
    across = lax.axis_size("x")
    width = CAP * group // across
    send, position = call(
        push_kernel,
        (
            jax.ShapeDtypeStruct((across, width * v + SUB, v), BF16),
            jax.ShapeDtypeStruct((entries,), jnp.int32),
        ),
        [SMEM, SMEM, HBM, HBM],
        (HBM, SMEM),
        (owners.T, slots.T, amps, intersections),
        4 * entries * cube * v,
        2 * cube * (pairs + entries + group * CAP),
        [
            pltpu.VMEM((pairs, v, v), BF16),
            pltpu.VMEM((pairs, neighbours, v, v), BF16),
            pltpu.VMEM((entries, v, v), BF16),
            pltpu.VMEM((across, SUB, v), BF16),
            pltpu.SMEM((group,), jnp.int32),
            pltpu.SemaphoreType.DMA((entries,)),
            pltpu.SemaphoreType.DMA((pairs,)),
            pltpu.SemaphoreType.DMA((pairs,)),
            pltpu.SemaphoreType.DMA,
        ],
        58,
    )
    recv = lax.all_to_all(send, "x", 0, 0, tiled=True)
    recv, opposite = lax.optimization_barrier((recv, opposite))
    asked = recv[:, width * v, :width].astype(jnp.int32)
    sums = call(
        sum_kernel,
        jax.ShapeDtypeStruct((group // across * pairs, v, v), BF16),
        [SMEM, VMEM],
        VMEM,
        (asked, recv),
        group * CAP * cube,
        2 * cube * group * CAP,
        [pltpu.VMEM((pairs, v, v), F32)],
        48,
    )
    incoming = lax.psum_scatter(sums, "z", scatter_dimension=0, tiled=True)
    asked, sums = lax.optimization_barrier((asked, sums))
    reply = call(
        reply_kernel,
        jax.ShapeDtypeStruct((across, width, v, v), BF16),
        [SMEM, SMEM] + [VMEM] * 7,
        VMEM,
        (
            asked, lax.axis_index("z").astype(jnp.int32).reshape(1),
            column, high, zfar, zup2, zdown2, zup1, zdown1,
        ),
        0,
        4 * cube * group * CAP,
        [pltpu.VMEM((depth * pairs, v, v), BF16)],
    )
    reply, blocks, opposite = lax.optimization_barrier((reply, blocks, opposite))
    arrived = lax.all_to_all(reply, "x", 0, 0, tiled=True)
    two = jnp.concatenate([blocks, opposite], axis=0)
    own = jnp.concatenate(
        [two, above, below, shift(two, "y", 1), shift(two, "y", -1)],
        axis=0,
    )
    other = lax.ppermute(own, "core", [(0, 1), (1, 0)])
    base = call(
        integral_kernel,
        jax.ShapeDtypeStruct((pairs, v, v), F32),
        [SMEM, SMEM] + [VMEM] * 5,
        VMEM,
        (domains.T, me.reshape(1), own, other, rotation, amps, energies),
        6 * pairs * blocks.shape[1] * cube,
        4 * own.size,
    )
    pulled = call(
        pull_kernel,
        jax.ShapeDtypeStruct((pairs, v, v), F32),
        [SMEM, pl.BlockSpec(memory_space=pl.ANY), VMEM],
        VMEM,
        (position, arrived.reshape(group * CAP, v, v), intersections),
        4 * entries * cube * v,
        2 * cube * (2 * entries + 2 * pairs),
        [pltpu.VMEM((entries, v, v), BF16), pltpu.SemaphoreType.DMA((entries,))],
    )
    lane = jnp.arange(ring * pairs, dtype=jnp.int32)
    spread = jnp.where(lane // pairs == me, jnp.tile(tiles, ring), 0).astype(BF16)
    note = jnp.broadcast_to(spread[None, :], (SUB, ring * pairs))
    new_amps, slabs = call(
        update_kernel,
        (
            jax.ShapeDtypeStruct((pairs, v, v), BF16),
            jax.ShapeDtypeStruct((ring, pairs + 1, SUB, v), BF16),
        ),
        [VMEM] * 7,
        (VMEM, VMEM),
        (incoming, amps, rotation, energies, base, pulled, note),
        6 * pairs * cube * v,
        2 * cube * 10 * pairs,
    )
    gathered = lax.all_to_all(slabs, AUX, 0, 0, tiled=True)
    tile_count = coeffs.shape[0] * group
    partial_sum = call(
        slab_kernel,
        jax.ShapeDtypeStruct((tile_count, SUB, v), BF16),
        [VMEM],
        VMEM,
        (gathered,),
        2 * tile_count * ring * pairs * SUB * v,
        4 * gathered.size,
        [pltpu.VMEM((ring * pairs * SUB, v), F32), pltpu.VMEM((tile_count, SUB, v), F32)],
    )
    spread_sum = lax.all_to_all(partial_sum, PAIR, 0, 0, tiled=True)
    slab = jnp.sum(spread_sum.astype(F32), axis=0).astype(BF16)
    whole = lax.all_to_all(
        jnp.broadcast_to(slab[None], (ring, SUB, v)), AUX, 0, 0, tiled=True
    ).reshape(v, v)
    factor = 1.0 / (pairs * ring)
    density = jnp.dot(whole, coeffs[0], preferred_element_type=F32) * factor
    return (new_amps, density[None])


def solution(mesh):
    fine = Mesh(mesh.devices.reshape(FINE), PAIR + AUX)

    return jax.shard_map(
        local,
        mesh=fine,
        in_specs=(
            P(PAIR + AUX, None, None),
            P(PAIR + AUX, None, None),
            P(PAIR + AUX, None, None, None),
            P(PAIR + AUX, None),
            P(PAIR + AUX, None),
            P(PAIR + AUX, None),
            P(PAIR + AUX, None),
            P(PAIR + AUX),
            P(AUX, None, None),
            P(PAIR, None, AUX),
        ),
        out_specs=(P(PAIR + AUX, None, None), P(PAIR, None, AUX)),
        check_vma=False,
    )
```

```python
import jax
import jax.numpy as jnp
from jax import lax
from jax.experimental import pallas as pl
from jax.experimental.pallas import tpu as pltpu
from jax.sharding import Mesh
from jax.sharding import PartitionSpec as P


F32 = jnp.float32
BF16 = jnp.bfloat16
CAP = 2
PAIR = ("x", "z")
AUX = ("y", "core")
FINE = (4, 8, 8, 2)
SUB = 8
CORES = 2
VMEM = pl.BlockSpec(memory_space=pltpu.VMEM)
SMEM = pl.BlockSpec(memory_space=pltpu.SMEM)
HBM = pl.BlockSpec(memory_space=pltpu.HBM)
PLACE = (0, 4, 2, 7, 1, 5, 3, 6)


def mm(a, b, ca=1, cb=0):
    return lax.dot_general(a, b, (((ca,), (cb,)), ((), ())), preferred_element_type=F32)


def call(kernel, out_shape, in_specs, out_specs, args, flops, bytes_accessed, scratch=(), mib=12):
    return pl.pallas_call(
        kernel,
        out_shape=out_shape,
        in_specs=in_specs,
        out_specs=out_specs,
        scratch_shapes=list(scratch),
        compiler_params=pltpu.CompilerParams(vmem_limit_bytes=mib << 20),
        cost_estimate=pl.CostEstimate(
            flops=flops, bytes_accessed=bytes_accessed, transcendentals=0
        ),
    )(*args)


def push_kernel(owner_ref, slot_ref, amps_ref, inter_ref, send_ref, pos_ref, *scratch):
    amps_buf, inter_buf, block_buf, note_buf, count, sems, amps_sems, inter_sems, note_sem = scratch
    pairs, neighbours, v, _ = inter_ref.shape
    rows = send_ref.shape[0]
    width = send_ref.shape[1] // v
    step = 2

    def get(p):
        return (
            pltpu.make_async_copy(amps_ref.at[p], amps_buf.at[p], amps_sems.at[p]),
            pltpu.make_async_copy(inter_ref.at[p], inter_buf.at[p], inter_sems.at[p]),
        )

    for p in range(pairs):
        for copy in get(p):
            copy.start()

    def put(e):
        at = pos_ref[e]
        place = pl.ds(pl.multiple_of(lax.rem(at, width) * v, v), v)
        return pltpu.make_async_copy(
            block_buf.at[e], send_ref.at[at // width, place, :], sems.at[e]
        )

    def put_notes():
        return pltpu.make_async_copy(note_buf, send_ref.at[:, pl.ds(width * v, SUB), :], note_sem)

    def put_all(g):
        for i in range(step * neighbours):
            put(g * step * neighbours + i).start()

    note_buf[...] = jnp.zeros(note_buf.shape, BF16)
    lane = lax.broadcasted_iota(jnp.int32, (SUB, v), 1)

    @pl.loop(0, rows * width // CAP)
    def _(o):
        count[o] = 0

    @pl.loop(0, pairs)
    def _(p):
        for n in range(neighbours):
            o = owner_ref[n, p]
            r = count[o]
            count[o] = r + 1
            at = o * CAP + r
            pos_ref[p * neighbours + n] = at
            d = at // width
            mark = jnp.where(lane == lax.rem(at, width), slot_ref[n, p] + 1, 0)
            note_buf[d] = note_buf[d] + mark.astype(F32).astype(BF16)

    @pl.loop(0, pairs // step)
    def _(g):
        for i in range(step):
            for copy in get(g * step + i):
                copy.wait()
        overs = [[inter_buf[g * step + i, n] for n in range(neighbours)] for i in range(step)]
        halves = [
            mm(jnp.concatenate(overs[i], axis=1), amps_buf[g * step + i], 0, 0).astype(BF16)
            for i in range(step)
        ]
        for i in range(step):
            for n in range(neighbours):
                block = mm(halves[i][n * v : (n + 1) * v, :], overs[i][n]).astype(BF16)
                block_buf[(g * step + i) * neighbours + n] = block

        @pl.when(g > 0)
        def _():
            put_all(g - 1)

    put_notes().start()
    put_all(pairs // step - 1)
    put_notes().wait()

    @pl.loop(0, pairs * neighbours)
    def _(e):
        put(e).wait()


def reply_kernel(want_ref, held_ref, out_ref):
    rows, width = want_ref.shape
    per = held_ref.shape[0] // (width // CAP)

    @pl.loop(0, rows)
    def _(d):
        for i in range(width):
            out_ref[d, i] = held_ref[i // CAP * per + jnp.maximum(want_ref[d, i] - 1, 0)]


def sum_kernel(want_ref, recv_ref, out_ref, total):
    rows, width = want_ref.shape
    per, v, _ = total.shape

    @pl.loop(0, width // CAP)
    def _(o):
        total[...] = jnp.zeros(total.shape, F32)
        for d in range(rows):
            for r in range(CAP):
                s = want_ref[d, o * CAP + r]
                place = pl.ds(pl.multiple_of((o * CAP + r) * v, v), v)

                @pl.when(s > 0)
                def _():
                    total[s - 1] += recv_ref[d, place, :].astype(F32)

        out_ref[pl.ds(o * per, per)] = total[...].astype(BF16)


def pack_kernel(*refs):
    out_ref = refs[-1]
    at = 0
    for ref in refs[:-1]:
        out_ref[at : at + ref.shape[0]] = ref[...]
        at += ref.shape[0]


def denominator(energy_ref, p):
    v = energy_ref.shape[1]
    across = jnp.broadcast_to(energy_ref[pl.ds(p, 1), :], (v, v))
    return across.T + across


def integral_kernel(
    domain_ref, me_ref, own_ref, other_ref, rot_ref, amps_ref, energy_ref, out_ref
):
    pairs = rot_ref.shape[0]
    per = own_ref.shape[0] // len(PLACE)
    chip = me_ref[0] // CORES
    core = lax.rem(me_ref[0], CORES)

    @pl.loop(0, pairs)
    def _(p):
        rot = rot_ref[p]

        def block(side):
            d = domain_ref[side, p]
            device = d // per
            back = lax.rem(chip - device // CORES + len(PLACE), len(PLACE))
            place = jnp.int32(PLACE[0])
            for k in range(1, len(PLACE)):
                place = jnp.where(back == k, PLACE[k], place)
            at = place * per + lax.rem(d, per)
            same = (lax.rem(device, CORES) == core).astype(jnp.int32)
            pick = jnp.full((1, 1), same) > 0
            return jnp.where(pick, own_ref[at], other_ref[at])

        left = mm(rot, block(0), 0, 1).astype(BF16)
        right = mm(block(1), rot).astype(BF16)
        amp = amps_ref[p].astype(F32)
        out_ref[p] = mm(left, right) + denominator(energy_ref, p) * amp


def pull_kernel(pos_ref, arrived_ref, inter_ref, out_ref, part, sems):
    pairs, neighbours, _, _ = inter_ref.shape
    step = 4

    def get(e):
        return pltpu.make_async_copy(arrived_ref.at[pos_ref[e]], part.at[e], sems.at[e])

    @pl.loop(0, pairs * neighbours)
    def _(e):
        get(e).start()

    @pl.loop(0, pairs // step)
    def _(g):
        at = [g * step + i for i in range(step)]
        for p in at:
            for n in range(neighbours):
                get(p * neighbours + n).wait()
        halves = [
            [
                mm(inter_ref[p, n], part[p * neighbours + n]).astype(BF16)
                for n in range(neighbours)
            ]
            for p in at
        ]
        for p, half in zip(at, halves):
            out_ref[p] = mm(
                jnp.concatenate(half, axis=1),
                jnp.concatenate([inter_ref[p, n] for n in range(neighbours)], axis=1),
                1,
                1,
            )


def update_kernel(
    incoming_ref, amps_ref, rot_ref, energy_ref, base_ref, pulled_ref, note_ref, new_ref, out_ref
):
    pairs, v, _ = amps_ref.shape
    slabs = out_ref.shape[0]
    step = 4

    for r in range(slabs):
        out_ref[r, pairs] = note_ref[...]

    @pl.loop(0, pairs // step)
    def _(g):
        at = [g * step + i for i in range(step)]
        news = []
        for p in at:
            residual = base_ref[p] - pulled_ref[p] - incoming_ref[p].astype(F32)
            amp = amps_ref[p].astype(F32)
            news.append((amp - residual / (denominator(energy_ref, p) + 1.0)).astype(BF16))
        densities = [(mm(new, new, 1, 1) * (1.0 / v)).astype(BF16) for new in news]
        rots = [mm(rot_ref[p], d).astype(BF16) for p, d in zip(at, densities)]
        for p, new, rotated in zip(at, news, rots):
            new_ref[p] = new
            tile = mm(rotated, rot_ref[p], 1, 1).astype(BF16)
            for r in range(slabs):
                out_ref[r, p] = tile[r * SUB : (r + 1) * SUB, :]


def slab_kernel(recv_ref, out_ref, wide, total):
    sources, blocks, _, _ = recv_ref.shape
    pairs = blocks - 1
    count = out_ref.shape[0]
    wide[...] = recv_ref[:, :pairs].astype(F32).reshape(wide.shape)
    ids = jnp.sum(recv_ref[:, pairs].astype(F32), axis=0)[0:1, :]
    which = lax.broadcasted_iota(jnp.int32, (count, sources * pairs), 0).astype(F32)
    hot = (which == ids).astype(F32).astype(BF16)
    for s in range(SUB):
        rows = wide[pl.ds(s, sources * pairs, stride=SUB), :].astype(BF16)
        total[:, s, :] = mm(hot, rows)
    out_ref[...] = total[...].astype(BF16)


def local(amps, rotation, intersections, energies, domains, owners, slots, tiles, blocks, coeffs):
    pairs, v, _ = amps.shape
    neighbours = owners.shape[1]
    group = lax.axis_size(PAIR)
    ring = lax.axis_size(AUX)
    chips = ring // CORES
    entries = pairs * neighbours
    cube = v * v
    me = lax.axis_index(AUX).astype(jnp.int32)

    assert chips == len(PLACE)

    def shift(value, axis, k):
        size = lax.axis_size(axis)
        return lax.ppermute(value, axis, [(j, (j + k) % size) for j in range(size)])

    opposite = shift(blocks, "y", 4)
    above, below = shift(blocks, "y", 2), shift(blocks, "y", -2)
    two = jnp.concatenate([blocks, opposite], axis=0)
    left, right = shift(two, "y", 1), shift(two, "y", -1)
    column = lax.all_gather(amps, "z", axis=0, tiled=True)
    across = lax.axis_size("x")
    width = CAP * group // across
    send, position = call(
        push_kernel,
        (
            jax.ShapeDtypeStruct((across, width * v + SUB, v), BF16),
            jax.ShapeDtypeStruct((entries,), jnp.int32),
        ),
        [SMEM, SMEM, HBM, HBM],
        (HBM, SMEM),
        (owners.T, slots.T, amps, intersections),
        4 * entries * cube * v,
        2 * cube * (pairs + entries + group * CAP),
        [
            pltpu.VMEM((pairs, v, v), BF16),
            pltpu.VMEM((pairs, neighbours, v, v), BF16),
            pltpu.VMEM((entries, v, v), BF16),
            pltpu.VMEM((across, SUB, v), BF16),
            pltpu.SMEM((group,), jnp.int32),
            pltpu.SemaphoreType.DMA((entries,)),
            pltpu.SemaphoreType.DMA((pairs,)),
            pltpu.SemaphoreType.DMA((pairs,)),
            pltpu.SemaphoreType.DMA,
        ],
        58,
    )
    recv = lax.all_to_all(send, "x", 0, 0, tiled=True)
    asked = recv[:, width * v, :width].astype(jnp.int32)
    sums = call(
        sum_kernel,
        jax.ShapeDtypeStruct((group // across * pairs, v, v), BF16),
        [SMEM, VMEM],
        VMEM,
        (asked, recv),
        group * CAP * cube,
        2 * cube * group * CAP,
        [pltpu.VMEM((pairs, v, v), F32)],
        48,
    )
    incoming = lax.psum_scatter(sums, "z", scatter_dimension=0, tiled=True)
    column, sums = lax.optimization_barrier((column, sums))
    reply = call(
        reply_kernel,
        jax.ShapeDtypeStruct((across, width, v, v), BF16),
        [SMEM, VMEM],
        VMEM,
        (asked, column),
        0,
        4 * cube * group * CAP,
    )
    arrived = lax.all_to_all(reply, "x", 0, 0, tiled=True)
    own = call(
        pack_kernel,
        jax.ShapeDtypeStruct((ring * blocks.shape[0] // CORES,) + blocks.shape[1:], BF16),
        [VMEM] * 5,
        VMEM,
        (two, above, below, left, right),
        0,
        4 * two.size * chips // 2,
    )
    other = lax.ppermute(own, "core", [(0, 1), (1, 0)])
    base = call(
        integral_kernel,
        jax.ShapeDtypeStruct((pairs, v, v), F32),
        [SMEM, SMEM] + [VMEM] * 5,
        VMEM,
        (domains.T, me.reshape(1), own, other, rotation, amps, energies),
        6 * pairs * blocks.shape[1] * cube,
        4 * own.size,
    )
    pulled = call(
        pull_kernel,
        jax.ShapeDtypeStruct((pairs, v, v), F32),
        [SMEM, pl.BlockSpec(memory_space=pl.ANY), VMEM],
        VMEM,
        (position, arrived.reshape(group * CAP, v, v), intersections),
        4 * entries * cube * v,
        2 * cube * (2 * entries + 2 * pairs),
        [pltpu.VMEM((entries, v, v), BF16), pltpu.SemaphoreType.DMA((entries,))],
    )
    lane = jnp.arange(ring * pairs, dtype=jnp.int32)
    spread = jnp.where(lane // pairs == me, jnp.tile(tiles, ring), 0).astype(BF16)
    note = jnp.broadcast_to(spread[None, :], (SUB, ring * pairs))
    new_amps, slabs = call(
        update_kernel,
        (
            jax.ShapeDtypeStruct((pairs, v, v), BF16),
            jax.ShapeDtypeStruct((ring, pairs + 1, SUB, v), BF16),
        ),
        [VMEM] * 7,
        (VMEM, VMEM),
        (incoming, amps, rotation, energies, base, pulled, note),
        6 * pairs * cube * v,
        2 * cube * 10 * pairs,
    )
    gathered = lax.all_to_all(slabs, AUX, 0, 0, tiled=True)
    tile_count = coeffs.shape[0] * group
    partial_sum = call(
        slab_kernel,
        jax.ShapeDtypeStruct((tile_count, SUB, v), BF16),
        [VMEM],
        VMEM,
        (gathered,),
        2 * tile_count * ring * pairs * SUB * v,
        4 * gathered.size,
        [pltpu.VMEM((ring * pairs * SUB, v), F32), pltpu.VMEM((tile_count, SUB, v), F32)],
    )
    spread_sum = lax.all_to_all(partial_sum, PAIR, 0, 0, tiled=True)
    slab = jnp.sum(spread_sum.astype(F32), axis=0).astype(BF16)
    whole = lax.all_to_all(
        jnp.broadcast_to(slab[None], (ring, SUB, v)), AUX, 0, 0, tiled=True
    ).reshape(v, v)
    factor = 1.0 / (pairs * ring)
    density = jnp.dot(whole, coeffs[0], preferred_element_type=F32) * factor
    return (new_amps, density[None])


def solution(mesh):
    fine = Mesh(mesh.devices.reshape(FINE), PAIR + AUX)

    return jax.shard_map(
        local,
        mesh=fine,
        in_specs=(
            P(PAIR + AUX, None, None),
            P(PAIR + AUX, None, None),
            P(PAIR + AUX, None, None, None),
            P(PAIR + AUX, None),
            P(PAIR + AUX, None),
            P(PAIR + AUX, None),
            P(PAIR + AUX, None),
            P(PAIR + AUX),
            P(AUX, None, None),
            P(PAIR, None, AUX),
        ),
        out_specs=(P(PAIR + AUX, None, None), P(PAIR, None, AUX)),
        check_vma=False,
    )
```
